256 devices in a mesh: grp: 2 (over core), pen: 16 (over x_lo, z), gz: 8 (over x_hi, y).
Axes of the slice: x: 4 (x_hi: 2, x_lo: 2; x = x_hi * 2 + x_lo), y: 4, z: 8, core: 2. Of those that a mesh axis runs over, the one named last changes fastest.
Arguments:
- velocity: float32 [4, 3, 16, 512, 256], P('grp', None, 'gz', 'pen'), may hold values from -6 to 6
- fringe_source: int32 [192], replicated, may hold values from 0 to 255
- blend_index: int32 [192], replicated, may hold values from 0 to 15
- blend_table: float32 [16], replicated, may hold values from 0.2 to 1
Outputs:
- velocity_next: float32 [4, 3, 16, 512, 256], P('grp', None, 'gz', 'pen')
The draws below stay inside these ranges and needn't reach their ends.
All inputs are finite; a program needn't handle non-finite values.
Results may differ from the reference program's by a relative error of at most 0.0003.
Values sent between devices are 32-bit elements; how exact they have to be, the bound alone decides.
No kernel may reach another device: no remote copies, remote signals or barrier semaphores. Data moves between devices by JAX's collectives and lax.ppermute only.
A program may use at most 64 MiB of HBM per device.

```python
import jax
import jax.numpy as jnp
from jax import lax

NB = 256
NY = 512
NFR = 192
NTAB = 16
NZ = 16
SPAN_DEV = 32


def touch_ends(values, own_key, least, top_value):
    place = [jax.random.randint(jax.random.fold_in(own_key, axis), (), 0, length) for axis, length in enumerate(values.shape)]
    main_axis = values.shape.index(max(values.shape))
    next_to = place[:main_axis] + [(place[main_axis] + 1) % values.shape[main_axis]] + place[main_axis + 1:]
    return values.at[tuple(place)].set(least).at[tuple(next_to)].set(top_value)


def shard_levels(key, extent, shards, smallest, high):
    factor_of, own = 1.0, jax.random.fold_in(key, 6)
    for position, parts in shards:
        steps = jnp.exp(jax.random.uniform(jax.random.fold_in(own, position), (parts,), jnp.float32, smallest / len(shards), high / len(shards)))
        factor_of = factor_of * jnp.repeat(steps, extent[position] // parts).reshape([-1 if axis == position else 1 for axis in range(len(extent))])
    return factor_of


def bell_draw(key, shape, deviation, reach, split=(), held_as=jnp.bfloat16):
    entries = deviation * jax.random.normal(key, shape, jnp.float32)
    if split:
        entries = entries * shard_levels(key, shape, split, -0.22, 0.18)
    return jnp.clip(entries, -reach, reach).astype(held_as)


def setup_inputs(seed: int = 0) -> dict:
    keys = jax.random.split(jax.random.key(seed), 5)
    return {
        "velocity": bell_draw(keys[0], (4, 3, NZ, NY, NB), 1.0, 6.0, ((0, 2), (2, 8), (3, 16)), jnp.float32),
        "fringe_source": touch_ends(jax.random.randint(keys[1], (NFR,), 0, NB), jax.random.fold_in(keys[1], 1), 0, NB - 1).astype(jnp.int32),
        "blend_index": touch_ends(jax.random.randint(keys[2], (NFR,), 0, NTAB), jax.random.fold_in(keys[2], 1), 0, NTAB - 1).astype(jnp.int32),
        "blend_table": jnp.clip(jax.random.uniform(keys[3], (NTAB,), jnp.float32, 0.2, 1.0), 0.2, 1.0),
    }


SMAGORINSKY = 0.04
TIMESTEP = 0.1

def natural_order(field):
    lead_shape = field.shape[:-2]
    row_count = field.shape[-2]
    cell_count = field.shape[-1]
    groups = row_count // SPAN_DEV
    split_rows = field.reshape(lead_shape + (groups, SPAN_DEV, cell_count))
    return jnp.swapaxes(split_rows, -3, -2).reshape(field.shape)

def stored_order(field):
    lead_shape = field.shape[:-2]
    row_count = field.shape[-2]
    cell_count = field.shape[-1]
    groups = row_count // SPAN_DEV
    split_rows = field.reshape(lead_shape + (SPAN_DEV, groups, cell_count))
    return jnp.swapaxes(split_rows, -3, -2).reshape(field.shape)

def spectral_derivative(values, axis_index):
    length = values.shape[axis_index]
    coeffs = jnp.fft.rfft(values, axis=axis_index)
    mode_list = jnp.arange(length // 2 + 1)
    wavenum = jnp.where(mode_list == length // 2, 0.0, 2.0 * jnp.pi * mode_list / length)
    shape_list = [1] * values.ndim
    shape_list[axis_index] = length // 2 + 1
    factor = (1j * wavenum).reshape(shape_list)
    return jnp.fft.irfft(coeffs * factor, n=length, axis=axis_index).astype(values.dtype)

def strain_terms(col_speed, gradients):
    strain = {}
    squares = jnp.zeros_like(col_speed[0])
    for comp_a in range(3):
        for comp_b in range(comp_a, 3):
            strain_value = 0.5 * (gradients[comp_b][comp_a] + gradients[comp_a][comp_b])
            strain[comp_a, comp_b] = strain_value
            strain[comp_b, comp_a] = strain_value
            weight_sq = 1.0 if comp_a == comp_b else 2.0
            squares = squares + weight_sq * strain_value * strain_value
    eddy_visc = SMAGORINSKY * jnp.sqrt(2.0 * squares)
    fluxes = [jnp.stack([2.0 * eddy_visc * strain[comp_a, comp_b] for comp_a in range(3)]) for comp_b in range(3)]
    advect = sum((col_speed[comp_b][None] * gradients[comp_b] for comp_b in range(3)))
    return (fluxes, advect)

def domain_tendency(domain_field):
    levels = domain_field.shape[1]
    padded = jnp.pad(domain_field, ((0, 0), (2, 2), (0, 0), (0, 0)))

    def one_level(level_id):
        window = lax.dynamic_slice_in_dim(padded, level_id, 5, 1)
        centre = window[:, 1:4]
        gradients = (spectral_derivative(centre, -1), spectral_derivative(centre, -2), 0.5 * (window[:, 2:5] - window[:, 0:3]))
        fluxes, advect = strain_terms(centre, gradients)
        heights = level_id - 1 + jnp.arange(3, dtype=jnp.int32)
        inside = ((heights >= 0) & (heights < levels)).astype(domain_field.dtype)[None, :, None, None]
        flux_z = fluxes[2] * inside
        result = spectral_derivative(fluxes[0][:, 1], -1) + spectral_derivative(fluxes[1][:, 1], -2)
        result = result + 0.5 * (flux_z[:, 2] - flux_z[:, 0]) - advect[:, 1]
        return result
    stacked = lax.map(one_level, jnp.arange(levels, dtype=jnp.int32))
    return jnp.transpose(stacked, (1, 0, 2, 3))

def reference(velocity, fringe_source, blend_index, blend_table):
    blocks = [natural_order(velocity[block_id]) for block_id in range(4)]
    block_shape = blocks[0].shape
    farm_field = jnp.stack(blocks[:3], axis=-1).reshape(block_shape[:-1] + (3 * block_shape[-1],))
    inflow = blocks[3]
    farm_step = farm_field + TIMESTEP * domain_tendency(farm_field)
    inflow_step = inflow + TIMESTEP * domain_tendency(inflow)
    weights = blend_table[blend_index]
    source = jnp.take(inflow_step, fringe_source, axis=-1)
    fringe_head = farm_step[..., :NFR]
    blended = jnp.concatenate([fringe_head + weights * (source - fringe_head), farm_step[..., NFR:]], axis=-1)
    farm_blocks = blended.reshape(block_shape + (3,))
    return jnp.stack([stored_order(farm_blocks[..., 0]), stored_order(farm_blocks[..., 1]), stored_order(farm_blocks[..., 2]), stored_order(inflow_step)])
```

```python
import functools

import jax
import jax.numpy as jnp
import ml_dtypes
import numpy as np
from jax import lax
from jax.experimental import pallas as pl
from jax.experimental.pallas import tpu as pltpu
from jax.sharding import PartitionSpec as P

SMAGORINSKY = 0.04
TIMESTEP = 0.1
F32 = jnp.float32
BF16 = jnp.bfloat16
WHOLE = pl.BlockSpec(memory_space=pltpu.VMEM)


def cotangent(offset, length):
    reduced = (offset + length // 2) % length - length // 2
    angle = np.pi * np.where(reduced == 0, 1, reduced) / length
    sign = np.where(reduced % 2 == 0, 1.0, -1.0)
    entry = sign * np.pi / length * np.cos(angle) / np.sin(angle)
    return np.where((reduced == 0) | (abs(reduced) == length // 2), 0.0, entry)


def split_table(table):
    table = table.astype(np.float32)
    high = table.astype(ml_dtypes.bfloat16)
    low = (table - high.astype(np.float32)).astype(ml_dtypes.bfloat16)
    return high, low


def span_table(devices, rows):
    length = devices * rows
    part = rows // 4
    p = np.repeat(np.arange(devices), part)
    s = np.tile(np.arange(part), devices)
    cell = s * devices + p
    quarters = [
        cotangent(j * (length // 4) + cell[:, None] - cell[None, :], length) for j in range(4)
    ]
    high, low = split_table(np.concatenate(quarters, axis=0))
    return np.concatenate([high, high, low], axis=1)


def stream_table(width):
    cell = np.arange(width)
    apart = cell[None, :] - cell[:, None]
    farm = [cotangent(3 * apart - shift, 3 * width) for shift in range(-2, 3)]
    tables = np.stack(farm + [cotangent(apart, width), np.zeros((width, width))])
    return split_table(tables)


STREAM_PICK = (
    (((2, 2), (3, 6), (4, 0), (6, 1))),
    (((1, 6), (2, 5), (3, 6), (6, 6))),
)


def halves(value):
    high = value.astype(BF16)
    low = (value - high.astype(F32)).astype(BF16)
    return high, low


def swap_groups(parts):
    lane = lax.broadcasted_iota(jnp.int32, parts[0].shape, 1)
    low64 = lane < 64
    even32 = (lane & 32) == 0
    a, b, c, d = parts

    def pair(left, right, keep, shift):
        return (
            jnp.where(keep, left, pltpu.roll(right, shift, 1)),
            jnp.where(keep, pltpu.roll(left, 128 - shift, 1), right),
        )

    a, c = pair(a, c, low64, 64)
    b, d = pair(b, d, low64, 64)
    a, b = pair(a, b, even32, 32)
    c, d = pair(c, d, even32, 32)
    return a, b, c, d


def pack_rows(block):
    chunks = []
    for half in range(2):
        chunks += swap_groups(
            [block[8 * q : 8 * q + 8, 128 * half : 128 * half + 128] for q in range(4)]
        )
    return chunks


def unpack_rows(chunks):
    lanes = []
    for half in range(2):
        lanes.append(jnp.concatenate(swap_groups(chunks[4 * half : 4 * half + 4]), axis=0))
    return jnp.concatenate(lanes, axis=1)


def span_derivative(table, lines):
    outs = []
    for at in range(0, len(lines), 2):
        group = jnp.concatenate(lines[at : at + 2], axis=1)
        high, low = halves(group)
        stacked = jnp.concatenate([high, low, high], axis=0)
        product = jnp.dot(table, stacked, preferred_element_type=F32)
        for side in range(len(lines[at : at + 2])):
            lanes = slice(128 * side, 128 * side + 128)
            total = product[0:128, lanes]
            for j in range(1, 4):
                total = total + pltpu.roll(product[128 * j : 128 * j + 128, lanes], 32 * j, 1)
            outs.append(total)
    return outs


def stream_derivative(sources, table_high, table_low, out_slot):
    group = lax.axis_index("grp")
    total = None
    for place, source in enumerate(sources):
        pick = STREAM_PICK[out_slot][place]
        entry = jnp.where(group == 0, pick[0], pick[1])
        high, low = source
        wide, fine = table_high[entry], table_low[entry]
        value = (
            jnp.dot(high, wide, preferred_element_type=F32)
            + jnp.dot(low, wide, preferred_element_type=F32)
            + jnp.dot(high, fine, preferred_element_type=F32)
        )
        total = value if total is None else total + value
    return total


def pack_kernel(u_ref, out_ref):
    for b in range(2):
        for c in range(3):
            for l in range(2):
                for at, chunk in enumerate(pack_rows(u_ref[b, c, l])):
                    out_ref[8 * b + at, c, l] = chunk


def stream_kernel(own_ref, peer_ref, high_ref, low_ref, out_ref):
    sources = [halves(ref[b].reshape(192, 256)) for ref in (own_ref, peer_ref) for b in range(2)]
    for slot in range(2):
        value = stream_derivative(sources, high_ref, low_ref, slot)
        out_ref[slot] = value.reshape(out_ref.shape[1:])


def level_difference(own_ref, below_ref, above_ref, b, c, l):
    if l == 0:
        return 0.5 * (own_ref[b, c, 1] - below_ref[b, c, 0])
    return 0.5 * (above_ref[b, c, 0] - own_ref[b, c, 0])


def terms_kernel(u_ref, below_ref, above_ref, gx_ref, gz_ref, out_ref):
    for b in range(2):
        for l in range(2):
            gz = [level_difference(u_ref, below_ref, above_ref, b, c, l) for c in range(3)]
            for c in range(3):
                gz_ref[b, c, l] = gz[c]
            s_xx = gx_ref[b, 0, l]
            s_xz = 0.5 * (gx_ref[b, 2, l] + gz[0])
            known = s_xx * s_xx + gz[2] * gz[2] + 2.0 * (s_xz * s_xz)
            for k, value in enumerate((known, gx_ref[b, 1, l], gz[1])):
                for at, chunk in enumerate(pack_rows(value)):
                    out_ref[8 * b + at, k, l] = chunk


def first_span_kernel(lines_ref, terms_ref, table_ref, out_ref):
    lines = [lines_ref[:, c, l].reshape(128, 128) for c in range(3) for l in range(2)]
    values = span_derivative(table_ref[...], lines)
    for c in range(3):
        for l in range(2):
            out_ref[:, c, l] = values[2 * c + l].reshape(16, 8, 128)
    out_ref[:, 3:6] = terms_ref[...]


def second_span_kernel(sent_ref, came_ref, table_ref, out_ref):
    lines = [None] * 6
    for l in range(2):
        s_xy = 0.5 * (came_ref[:, 4, l] + sent_ref[:, 0, l])
        s_yy = sent_ref[:, 1, l]
        s_yz = 0.5 * (came_ref[:, 5, l] + sent_ref[:, 2, l])
        squares = came_ref[:, 3, l] + s_yy * s_yy + 2.0 * (s_xy * s_xy + s_yz * s_yz)
        twice = (2.0 * SMAGORINSKY) * jnp.sqrt(2.0 * squares)
        for c, strain in enumerate((s_xy, s_yy, s_yz)):
            lines[2 * c + l] = (twice * strain).reshape(128, 128)
    values = span_derivative(table_ref[...], lines)
    for c in range(3):
        for l in range(2):
            out_ref[:, c, l] = values[2 * c + l].reshape(16, 8, 128)


def stress_kernel(u_ref, gx_ref, gz_ref, came_ref, tx_ref, tz_ref, rest_ref):
    for b in range(2):
        for l in range(2):
            gx = [gx_ref[b, c, l] for c in range(3)]
            gz = [gz_ref[b, c, l] for c in range(3)]
            gy = [unpack_rows([came_ref[8 * b + at, c, l] for at in range(8)]) for c in range(3)]
            s_xy = 0.5 * (gx[1] + gy[0])
            s_xz = 0.5 * (gx[2] + gz[0])
            s_yz = 0.5 * (gy[2] + gz[1])
            squares = (
                gx[0] * gx[0]
                + gy[1] * gy[1]
                + gz[2] * gz[2]
                + 2.0 * (s_xy * s_xy + s_xz * s_xz + s_yz * s_yz)
            )
            twice = (2.0 * SMAGORINSKY) * jnp.sqrt(2.0 * squares)
            for c, strain in enumerate((gx[0], s_xy, s_xz)):
                tx_ref[b, c, l] = twice * strain
            for c, strain in enumerate((s_xz, s_yz, gz[2])):
                tz_ref[b, c, l] = twice * strain
            u = [u_ref[b, c, l] for c in range(3)]
            for c in range(3):
                advect = u[0] * gx[c] + u[1] * gy[c] + u[2] * gz[c]
                rest_ref[b, c, l] = u[c] - TIMESTEP * advect


def gather_kernel(rest_ref, tz_ref, below_ref, above_ref, own_ref, peer_ref, high_ref, low_ref, out_ref):
    sources = [halves(ref[b].reshape(192, 256)) for ref in (own_ref, peer_ref) for b in range(2)]
    for b in range(2):
        value = stream_derivative(sources, high_ref, low_ref, b).reshape(out_ref.shape[1:])
        for c in range(3):
            for l in range(2):
                lift = level_difference(tz_ref, below_ref, above_ref, b, c, l)
                out_ref[b, c, l] = rest_ref[b, c, l] + TIMESTEP * (value[c, l] + lift)


def step_kernel(base_ref, came_ref, source_ref, out_ref, planes_ref):
    for b in range(2):
        for c in range(3):
            for l in range(2):
                flux = unpack_rows([came_ref[8 * b + at, c, l] for at in range(8)])
                out_ref[b, c, l] = base_ref[b, c, l] + TIMESTEP * flux
    inflow = out_ref[1].reshape(192, 256)
    cell = lax.broadcasted_iota(jnp.int32, (256, 256), 0)
    chosen = jnp.where(cell == source_ref[...], 1.0, 0.0).astype(BF16)
    high, low = halves(inflow)
    rest = (inflow - high.astype(F32) - low.astype(F32)).astype(BF16)
    planes = (
        jnp.dot(high, chosen, preferred_element_type=F32)
        + jnp.dot(low, chosen, preferred_element_type=F32)
        + jnp.dot(rest, chosen, preferred_element_type=F32)
    )
    planes_ref[0] = planes[:, :128].reshape(planes_ref.shape[1:])
    planes_ref[1] = planes[:, 128:].reshape(planes_ref.shape[1:])


def blend_kernel(step_ref, came_ref, planes_ref, weight_ref, out_ref):
    first = lax.axis_index("grp") == 0
    for c in range(3):
        for l in range(2):
            head = step_ref[0, c, l]
            came = came_ref[c, l]
            source = jnp.where(first, came, planes_ref[1, c, l])
            out_ref[0, c, l] = head + weight_ref[0:1] * (source - head)
            head = step_ref[1, c, l]
            source = pltpu.roll(came, 64, 1)
            out_ref[1, c, l] = head + weight_ref[1:2] * (source - head)


def call(kernel, shapes, count, **more):
    many = isinstance(shapes, list)
    return pl.pallas_call(
        kernel,
        out_shape=[jax.ShapeDtypeStruct(s, F32) for s in shapes]
        if many
        else jax.ShapeDtypeStruct(shapes, F32),
        in_specs=[WHOLE] * count,
        out_specs=[WHOLE] * len(shapes) if many else WHOLE,
        **more,
    )


def transpose_pen(value):
    return lax.all_to_all(value, "pen", 0, 0, tiled=True)


def swap_grp(value):
    return lax.ppermute(value, "grp", [(0, 1), (1, 0)])


def level_ends(value):
    count = lax.axis_size("gz")
    below = lax.ppermute(value[:, :, 1:2], "gz", [(i, i + 1) for i in range(count - 1)])
    above = lax.ppermute(value[:, :, 0:1], "gz", [(i + 1, i) for i in range(count - 1)])
    return below, above


def per_device(velocity, fringe_source, blend_index, blend_table):
    shape = velocity.shape
    span = jnp.asarray(span_table(16, 32))
    high, low = (jnp.asarray(t) for t in stream_table(256))
    chunks = (16, 3, 2, 8, 128)

    sent = call(pack_kernel, chunks, 1)(velocity)
    lines = transpose_pen(sent)
    peer = swap_grp(velocity)
    below, above = level_ends(velocity)
    grad_x = call(stream_kernel, shape, 4)(velocity, peer, high, low)
    grad_z, terms = call(terms_kernel, [shape, chunks], 4)(velocity, below, above, grad_x)
    sent = call(first_span_kernel, (16, 6, 2, 8, 128), 3)(lines, terms, span)
    came = transpose_pen(sent)
    flux_sent = call(second_span_kernel, chunks, 3)(sent, came, span)
    flux_y = transpose_pen(flux_sent)
    flux_x, flux_z, rest = call(stress_kernel, [shape] * 3, 4)(velocity, grad_x, grad_z, came)
    flux_peer = swap_grp(flux_x)
    below, above = level_ends(flux_z)
    base = call(gather_kernel, shape, 8)(
        rest, flux_z, below, above, flux_x, flux_peer, high, low
    )

    third = fringe_source.shape[0] // 3
    source = fringe_source.reshape(third, 3).T.reshape(1, 3 * third)
    source = jnp.pad(source, ((0, 0), (0, 256 - 3 * third)), constant_values=-1)
    entries = jnp.arange(blend_table.shape[0], dtype=jnp.int32)
    weight = jnp.sum(
        jnp.where(blend_index[:, None] == entries[None, :], blend_table[None, :], 0.0), axis=1
    )
    weight = weight.reshape(third, 3).T
    group = lax.axis_index("grp")
    slots = jnp.where(
        group == 0, weight[0:2], jnp.stack([weight[2], jnp.zeros_like(weight[2])])
    )
    slots = jnp.pad(slots, ((0, 0), (0, 128 - third)))

    stepped, planes = call(step_kernel, [shape, (2, 3, 2, 32, 128)], 3)(base, flux_y, source)
    arrived = lax.ppermute(planes[0], "grp", [(1, 0)])
    half = pl.BlockSpec((2, 3, 2, 32, 128), lambda i: (0, 0, 0, 0, 0))
    return pl.pallas_call(
        blend_kernel,
        grid=(1,),
        out_shape=jax.ShapeDtypeStruct(shape, F32),
        in_specs=[half, WHOLE, WHOLE, WHOLE],
        out_specs=half,
        input_output_aliases={0: 0},
    )(stepped, arrived, planes, slots)


def solution(mesh):
    placed = (P("grp", None, "gz", "pen", None), P(), P(), P())
    return jax.shard_map(
        per_device,
        mesh=mesh,
        in_specs=placed,
        out_specs=P("grp", None, "gz", "pen", None),
        check_vma=False,
    )
```

```python
import functools

import jax
import jax.numpy as jnp
import ml_dtypes
import numpy as np
from jax import lax
from jax.experimental import pallas as pl
from jax.experimental.pallas import tpu as pltpu
from jax.sharding import PartitionSpec as P

SMAGORINSKY = 0.04
TIMESTEP = 0.1
F32 = jnp.float32
BF16 = jnp.bfloat16
WHOLE = pl.BlockSpec(memory_space=pltpu.VMEM)


def cotangent(offset, length):
    reduced = (offset + length // 2) % length - length // 2
    angle = np.pi * np.where(reduced == 0, 1, reduced) / length
    sign = np.where(reduced % 2 == 0, 1.0, -1.0)
    entry = sign * np.pi / length * np.cos(angle) / np.sin(angle)
    return np.where((reduced == 0) | (abs(reduced) == length // 2), 0.0, entry)


def split_table(table):
    table = table.astype(np.float32)
    high = table.astype(ml_dtypes.bfloat16)
    low = (table - high.astype(np.float32)).astype(ml_dtypes.bfloat16)
    return high, low


def span_table(devices, rows):
    length = devices * rows
    part = rows // 4
    p = np.repeat(np.arange(devices), part)
    s = np.tile(np.arange(part), devices)
    cell = s * devices + p
    quarters = [
        cotangent(j * (length // 4) + cell[:, None] - cell[None, :], length) for j in range(4)
    ]
    high, low = split_table(np.concatenate(quarters, axis=0))
    return np.concatenate([high, high, low], axis=1)


def stream_table(width):
    cell = np.arange(width)
    apart = cell[None, :] - cell[:, None]
    farm = {k: cotangent(3 * apart - k, 3 * width) for k in range(-2, 3)}
    alone = cotangent(apart, width)
    sides = [[farm[0], farm[1], farm[2], farm[-1]], [farm[0], farm[-2], farm[-1], alone]]
    return np.stack(split_table(np.stack([np.stack(side) for side in sides])), axis=2)


def halves(value):
    high = value.astype(BF16)
    low = (value - high.astype(F32)).astype(BF16)
    return high, low


def swap_groups(parts):
    lane = lax.broadcasted_iota(jnp.int32, parts[0].shape, 1)
    low64 = lane < 64
    even32 = (lane & 32) == 0
    a, b, c, d = parts

    def pair(left, right, keep, shift):
        return (
            jnp.where(keep, left, pltpu.roll(right, shift, 1)),
            jnp.where(keep, pltpu.roll(left, 128 - shift, 1), right),
        )

    a, c = pair(a, c, low64, 64)
    b, d = pair(b, d, low64, 64)
    a, b = pair(a, b, even32, 32)
    c, d = pair(c, d, even32, 32)
    return a, b, c, d


def pack_rows(block):
    chunks = []
    for half in range(2):
        chunks += swap_groups(
            [block[8 * q : 8 * q + 8, 128 * half : 128 * half + 128] for q in range(4)]
        )
    return chunks


def unpack_rows(chunks):
    lanes = []
    for half in range(2):
        lanes.append(jnp.concatenate(swap_groups(chunks[4 * half : 4 * half + 4]), axis=0))
    return jnp.concatenate(lanes, axis=1)


def span_derivative(table, lines):
    outs = []
    for at in range(0, len(lines), 2):
        group = jnp.concatenate(lines[at : at + 2], axis=1)
        high, low = halves(group)
        stacked = jnp.concatenate([high, low, high], axis=0)
        product = jnp.dot(table, stacked, preferred_element_type=F32)
        for side in range(len(lines[at : at + 2])):
            lanes = slice(128 * side, 128 * side + 128)
            total = product[0:128, lanes]
            for j in range(1, 4):
                total = total + pltpu.roll(product[128 * j : 128 * j + 128, lanes], 32 * j, 1)
            outs.append(total)
    return outs


def stream_derivative(own, peer, table, store):
    def source(ref, b):
        return halves(ref[b].reshape(192, 256))

    def times(pair, at):
        high, low = pair
        wide, fine = table[at, 0], table[at, 1]
        return (
            jnp.dot(high, wide, preferred_element_type=F32)
            + jnp.dot(low, wide, preferred_element_type=F32)
            + jnp.dot(high, fine, preferred_element_type=F32)
        )

    group = lax.axis_index("grp")

    @pl.when(group == 0)
    def _():
        parts = [source(own, 0), source(own, 1), source(peer, 0)]
        store(0, times(parts[0], 0) + times(parts[1], 1) + times(parts[2], 2))
        store(1, times(parts[0], 3) + times(parts[1], 0) + times(parts[2], 1))

    @pl.when(group == 1)
    def _():
        parts = [source(own, 0), source(peer, 0), source(peer, 1)]
        store(0, times(parts[0], 0) + times(parts[1], 1) + times(parts[2], 2))
        store(1, times(source(own, 1), 3))


def pack_kernel(u_any, out_any, low_ref, high_ref, u_ref, out_ref, in_sem, out_sem):
    def load(b, c):
        return pltpu.make_async_copy(u_any.at[b, c], u_ref.at[b, c], in_sem.at[3 * b + c])

    def save(b, c):
        rows = pl.ds(8 * b, 8)
        return pltpu.make_async_copy(
            out_ref.at[rows, c], out_any.at[rows, c], out_sem.at[3 * b + c]
        )

    places = [(b, c) for b in range(2) for c in range(3)]
    for place in places:
        load(*place).start()
    for b, c in places:
        load(b, c).wait()
        for l in range(2):
            for at, chunk in enumerate(pack_rows(u_ref[b, c, l])):
                out_ref[8 * b + at, c, l] = chunk
        save(b, c).start()
        low_ref[b, c] = u_ref[b, c, 0]
        high_ref[b, c] = u_ref[b, c, 1]
    for place in places:
        save(*place).wait()


def stream_kernel(own_any, peer_ref, table_any, out_ref, own_ref, table_ref, own_sem, sem):
    load = [pltpu.make_async_copy(own_any.at[b], own_ref.at[b], own_sem.at[b]) for b in range(2)]
    for copy in load:
        copy.start()
    fetch_table(table_any, table_ref, sem)
    for copy in load:
        copy.wait()

    def store(slot, value):
        out_ref[slot] = value.reshape(out_ref.shape[1:])

    stream_derivative(own_ref, peer_ref, table_ref, store)


def fetch_table(table_any, table_ref, sem):
    group = lax.axis_index("grp")
    copies = [
        pltpu.make_async_copy(table_any.at[group, k], table_ref.at[k], sem.at[k])
        for k in range(4)
    ]
    for copy in copies:
        copy.start()
    for copy in copies:
        copy.wait()


def terms_kernel(low_ref, high_ref, below_ref, above_ref, gx_ref, gx_any, gz_any, out_ref, gz_ref, sem):
    save = [pltpu.make_async_copy(gx_ref.at[b], gx_any.at[b], sem.at[b]) for b in range(2)]
    save += [pltpu.make_async_copy(gz_ref.at[b], gz_any.at[b], sem.at[2 + b]) for b in range(2)]
    save[0].start()
    save[1].start()
    for b in range(2):
        for l in range(2):
            gz = [
                0.5 * (high_ref[b, c] - below_ref[b, c])
                if l == 0
                else 0.5 * (above_ref[b, c] - low_ref[b, c])
                for c in range(3)
            ]
            for c in range(3):
                gz_ref[b, c, l] = gz[c]
            s_xx = gx_ref[b, 0, l]
            s_xz = 0.5 * (gx_ref[b, 2, l] + gz[0])
            known = s_xx * s_xx + gz[2] * gz[2] + 2.0 * (s_xz * s_xz)
            for k, value in enumerate((known, gx_ref[b, 1, l], gz[1])):
                for at, chunk in enumerate(pack_rows(value)):
                    out_ref[8 * b + at, k, l] = chunk
        save[2 + b].start()
    for copy in save:
        copy.wait()


def first_span_kernel(lines_ref, terms_ref, table_ref, out_any, out_ref, sem):
    save = [
        pltpu.make_async_copy(out_ref.at[:, c], out_any.at[:, c], sem.at[c]) for c in range(3)
    ] + [
        pltpu.make_async_copy(terms_ref.at[:, c], out_any.at[:, 3 + c], sem.at[3 + c])
        for c in range(3)
    ]
    for copy in save[3:]:
        copy.start()
    lines = [lines_ref[:, c, l].reshape(128, 128) for c in range(3) for l in range(2)]
    for c in range(3):
        values = span_derivative(table_ref[...], lines[2 * c : 2 * c + 2])
        for l in range(2):
            out_ref[:, c, l] = values[l].reshape(16, 8, 128)
        save[c].start()
    for copy in save:
        copy.wait()


def second_span_kernel(sent_ref, came_ref, table_ref, out_any, out_ref, sem):
    save = [
        pltpu.make_async_copy(out_ref.at[:, c], out_any.at[:, c], sem.at[c]) for c in range(3)
    ]
    lines = [None] * 6
    for l in range(2):
        s_xy = 0.5 * (came_ref[:, 4, l] + sent_ref[:, 0, l])
        s_yy = sent_ref[:, 1, l]
        s_yz = 0.5 * (came_ref[:, 5, l] + sent_ref[:, 2, l])
        squares = came_ref[:, 3, l] + s_yy * s_yy + 2.0 * (s_xy * s_xy + s_yz * s_yz)
        twice = (2.0 * SMAGORINSKY) * jnp.sqrt(2.0 * squares)
        for c, strain in enumerate((s_xy, s_yy, s_yz)):
            lines[2 * c + l] = (twice * strain).reshape(128, 128)
    for c in range(3):
        values = span_derivative(table_ref[...], lines[2 * c : 2 * c + 2])
        for l in range(2):
            out_ref[:, c, l] = values[l].reshape(16, 8, 128)
        save[c].start()
    for copy in save:
        copy.wait()


def stress_kernel(u_any, gx_any, gz_any, came_ref, tx_ref, low_ref, high_ref, rest_ref, u_ref, gx_ref, gz_ref, sem):
    pairs = ((gx_any, gx_ref), (gz_any, gz_ref), (u_any, u_ref))
    load = [
        [pltpu.make_async_copy(f.at[b], t.at[b], sem.at[3 * b + k]) for k, (f, t) in enumerate(pairs)]
        for b in range(2)
    ]
    for copy in load[0] + load[1]:
        copy.start()
    for b in range(2):
        for copy in load[b]:
            copy.wait()
        for l in range(2):
            gx = [gx_ref[b, c, l] for c in range(3)]
            gz = [gz_ref[b, c, l] for c in range(3)]
            gy = [unpack_rows([came_ref[8 * b + at, c, l] for at in range(8)]) for c in range(3)]
            s_xy = 0.5 * (gx[1] + gy[0])
            s_xz = 0.5 * (gx[2] + gz[0])
            s_yz = 0.5 * (gy[2] + gz[1])
            squares = (
                gx[0] * gx[0]
                + gy[1] * gy[1]
                + gz[2] * gz[2]
                + 2.0 * (s_xy * s_xy + s_xz * s_xz + s_yz * s_yz)
            )
            twice = (2.0 * SMAGORINSKY) * jnp.sqrt(2.0 * squares)
            for c, strain in enumerate((gx[0], s_xy, s_xz)):
                tx_ref[b, c, l] = twice * strain
            side_ref = high_ref if l else low_ref
            for c, strain in enumerate((s_xz, s_yz, gz[2])):
                side_ref[b, c] = twice * strain
            u = [u_ref[b, c, l] for c in range(3)]
            for c in range(3):
                advect = u[0] * gx[c] + u[1] * gy[c] + u[2] * gz[c]
                rest_ref[b, c, l] = u[c] - TIMESTEP * advect


def gather_kernel(rest_ref, own_ref, peer_ref, table_any, out_ref, table_ref, sem):
    fetch_table(table_any, table_ref, sem)

    def store(slot, value):
        out_ref[slot] = rest_ref[slot] + TIMESTEP * value.reshape(out_ref.shape[1:])

    stream_derivative(own_ref, peer_ref, table_ref, store)


def stepped(b, base_ref, came_ref, low_ref, high_ref, below_ref, above_ref, c, l):
    flux = unpack_rows([came_ref[8 * b + at, c, l] for at in range(8)])
    if l == 0:
        lift = 0.5 * (high_ref[b, c] - below_ref[b, c])
    else:
        lift = 0.5 * (above_ref[b, c] - low_ref[b, c])
    return base_ref[b, c, l] + TIMESTEP * (flux + lift)


def inflow_kernel(base_ref, came_ref, low_ref, high_ref, below_ref, above_ref, source_ref, out_ref, sent_ref, kept_ref):
    for c in range(3):
        for l in range(2):
            out_ref[c, l] = stepped(
                1, base_ref, came_ref, low_ref, high_ref, below_ref, above_ref, c, l
            )
    inflow = out_ref[...].reshape(192, 256)
    cell = lax.broadcasted_iota(jnp.int32, (256, 256), 0)
    chosen = jnp.where(cell == source_ref[...], 1.0, 0.0).astype(BF16)
    high, low = halves(inflow)
    rest = (inflow - high.astype(F32) - low.astype(F32)).astype(BF16)
    planes = (
        jnp.dot(high, chosen, preferred_element_type=F32)
        + jnp.dot(low, chosen, preferred_element_type=F32)
        + jnp.dot(rest, chosen, preferred_element_type=F32)
    )
    sent_ref[...] = planes[:, :128].reshape(sent_ref.shape)
    kept_ref[...] = planes[:, 128:].reshape(kept_ref.shape)


def farm_kernel(base_ref, came_ref, low_ref, high_ref, below_ref, above_ref, inflow_ref, out_any, head_ref, tail_ref, sem):
    tail_ref[1] = inflow_ref[:, :, :, 128:]
    copies = [
        pltpu.make_async_copy(tail_ref.at[b], out_any.at[b, :, :, :, 128:256], sem.at[b])
        for b in range(2)
    ]
    copies[1].start()
    for c in range(3):
        for l in range(2):
            value = stepped(0, base_ref, came_ref, low_ref, high_ref, below_ref, above_ref, c, l)
            head_ref[c, l] = value[:, :128]
            tail_ref[0, c, l] = value[:, 128:]
    copies[0].start()
    copies[0].wait()
    copies[1].wait()


def blend_kernel(head_ref, inflow_ref, came_ref, kept_ref, weight_ref, made_any, out_any, done_ref, sem):
    first = lax.axis_index("grp") == 0
    copies = [
        pltpu.make_async_copy(done_ref.at[b], out_any.at[b, :, :, :, 0:128], sem.at[b])
        for b in range(2)
    ]
    for c in range(3):
        for l in range(2):
            head = head_ref[c, l]
            source = jnp.where(first, came_ref[c, l], kept_ref[c, l])
            done_ref[0, c, l] = head + weight_ref[0:1] * (source - head)
    copies[0].start()
    for c in range(3):
        for l in range(2):
            head = inflow_ref[c, l, :, :128]
            source = pltpu.roll(came_ref[c, l], 64, 1)
            done_ref[1, c, l] = head + weight_ref[1:2] * (source - head)
    copies[1].start()
    copies[0].wait()
    copies[1].wait()


FAR = pl.BlockSpec(memory_space=pltpu.HBM)


def placed(value, far):
    return pltpu.with_memory_space_constraint(value, pltpu.HBM if far else pltpu.VMEM)


def call(kernel, outs, operands, far=(), far_out=(), scratch=(), **more):
    return pl.pallas_call(
        kernel,
        out_shape=[
            (pltpu.HBM if at in far_out else pltpu.VMEM)(s, F32) for at, s in enumerate(outs)
        ],
        in_specs=[FAR if at in far else WHOLE for at in range(len(operands))],
        out_specs=[FAR if at in far_out else WHOLE for at in range(len(outs))],
        scratch_shapes=list(scratch),
        compiler_params=pltpu.CompilerParams(vmem_limit_bytes=16 << 20),
        **more,
    )(*[placed(value, at in far) for at, value in enumerate(operands)])


def transpose_pen(value):
    return lax.all_to_all(value, "pen", 0, 0, tiled=True)


def swap_grp(value):
    return lax.ppermute(value, "grp", [(0, 1), (1, 0)])


def level_ends(low, high):
    count = lax.axis_size("gz")
    below = lax.ppermute(high, "gz", [(i, i + 1) for i in range(count - 1)])
    above = lax.ppermute(low, "gz", [(i + 1, i) for i in range(count - 1)])
    return below, above


def fringe_arrays(fringe_source, blend_index, blend_table):
    third = fringe_source.shape[0] // 3
    source = fringe_source.reshape(third, 3).T.reshape(1, 3 * third)
    source = jnp.pad(source, ((0, 0), (0, 256 - 3 * third)), constant_values=-1)
    entries = jnp.arange(blend_table.shape[0], dtype=jnp.int32)
    weight = jnp.sum(
        jnp.where(blend_index[:, None] == entries[None, :], blend_table[None, :], 0.0), axis=1
    )
    weight = weight.reshape(third, 3).T
    group = lax.axis_index("grp")
    slots = jnp.where(
        group == 0, weight[0:2], jnp.stack([weight[2], jnp.zeros_like(weight[2])])
    )
    return source, jnp.pad(slots, ((0, 0), (0, 128 - third)))


def per_device(velocity, fringe_source, blend_index, blend_table):
    shape = velocity.shape
    level = (2, 3, 32, 256)
    planes = (3, 2, 32, 128)
    chunks = (16, 3, 2, 8, 128)
    span = jnp.asarray(span_table(16, 32))
    stream = jnp.asarray(stream_table(256))
    dma = pltpu.SemaphoreType.DMA
    table_scratch = [pltpu.VMEM((4, 2, 256, 256), BF16), dma((4,))]

    sent, low, high = call(
        pack_kernel,
        [chunks, level, level],
        [velocity],
        far=(0,),
        far_out=(0,),
        scratch=[pltpu.VMEM(shape, F32), pltpu.VMEM(chunks, F32), dma((6,)), dma((6,))],
    )
    lines = transpose_pen(sent)
    peer = swap_grp(velocity)
    below, above = level_ends(low, high)
    whole = pltpu.VMEM(shape, F32)
    (grad_x,) = call(
        stream_kernel,
        [shape],
        [velocity, peer, stream],
        far=(0, 2),
        scratch=[whole, table_scratch[0], dma((2,)), table_scratch[1]],
    )
    grad_x, grad_z, terms = call(
        terms_kernel,
        [shape, shape, chunks],
        [low, high, below, above, grad_x],
        far_out=(0, 1),
        scratch=[whole, dma((4,))],
    )
    sent, grad_y = call(
        first_span_kernel,
        [(16, 6, 2, 8, 128), chunks],
        [lines, terms, span],
        far_out=(0,),
        scratch=[dma((6,))],
    )
    sent, fringe = lax.optimization_barrier((sent, (fringe_source, blend_index, blend_table)))
    came = transpose_pen(sent)
    source, slots = fringe_arrays(*fringe)
    (flux_sent,) = call(
        second_span_kernel,
        [chunks],
        [grad_y, came, span],
        far_out=(0,),
        scratch=[pltpu.VMEM(chunks, F32), dma((3,))],
    )
    flux_sent, source, slots = lax.optimization_barrier((flux_sent, source, slots))
    flux_y = transpose_pen(flux_sent)
    flux_x, low, high, rest = call(
        stress_kernel,
        [shape, level, level, shape],
        [velocity, grad_x, grad_z, came],
        far=(0, 1, 2),
        scratch=[whole, whole, whole, dma((6,))],
    )
    below, above = level_ends(low, high)
    flux_peer = swap_grp(flux_x)
    (base,) = call(
        gather_kernel, [shape], [rest, flux_x, flux_peer, stream], far=(3,), scratch=table_scratch
    )

    ends = [low, high, below, above]
    inflow, planes_sent, planes_kept = call(
        inflow_kernel, [planes[:3] + (256,), planes, planes], [base, flux_y, *ends, source]
    )
    arrived = lax.ppermute(planes_sent, "grp", [(1, 0)])
    half = pltpu.VMEM((2,) + planes, F32)
    made, heads = call(
        farm_kernel,
        [shape, planes],
        [base, flux_y, *ends, inflow],
        far_out=(0,),
        scratch=[half, dma((2,))],
    )
    (result,) = call(
        blend_kernel,
        [shape],
        [heads, inflow, arrived, planes_kept, slots, made],
        far=(5,),
        far_out=(0,),
        scratch=[half, dma((2,))],
        input_output_aliases={5: 0},
    )
    return result


def solution(mesh):
    placed = (P("grp", None, "gz", "pen", None), P(), P(), P())
    return jax.shard_map(
        per_device,
        mesh=mesh,
        in_specs=placed,
        out_specs=P("grp", None, "gz", "pen", None),
        check_vma=False,
    )
```
